256 devices in a mesh: rows: 32 (over z, y), span: 8 (over x, core).
Axes of the slice: x: 4, y: 4, z: 8, core: 2. Of those that a mesh axis runs over, the one named last changes fastest.
Arguments:
- rotor_face: bfloat16 [8, 256, 160, 128], P('span', 'rows'), may hold values from -6 to 6
- pair_source: int32 [8, 1024, 1], P('span', 'rows'), may hold values from 0 to 31; in each aligned block of 32 rows (0 to 31, 32 to 63, ..., all dimensions but the last counted through in order) at most 2 rows name the same one
- pair_block: int32 [8, 1024], P('span', 'rows'), may hold values from 0 to 7
- pair_row: int32 [8, 1024], P('span', 'rows'), may hold values from 0 to 7
- pair_weight: bfloat16 [8, 1024, 128, 128], P('span', 'rows'), may hold values from -0.5 to 0.5
- stator_field: float32 [4, 160, 64, 4096], P(None, None, 'span', 'rows'), may hold values from -6 to 6
- damping: float32 [64, 4096], P('span', 'rows'), may hold values from 0.05 to 0.5
Outputs:
- interface: float32 [160, 64, 4096], P(None, 'span', 'rows')
- updated: float32 [4, 160, 64, 4096], P(None, None, 'span', 'rows')
The draws below stay inside these ranges and needn't reach their ends.
Inputs may be any that keep to these rules, and one draw needn't show every extreme that they name: `pair_source`: among the pairs of one receiving device, no source index appears more than 2 times; in every draw some device names one source exactly 2 times.
All inputs are finite; a program needn't handle non-finite values.
Results may differ from the reference program's by a relative error of at most 0.0003.
Values may be sent and summed in bfloat16 or wider, within the bound.
No kernel may reach another device: no remote copies, remote signals or barrier semaphores. Data moves between devices by JAX's collectives and lax.ppermute only.
A program may use at most 128 MiB of HBM per device.

```python
import math
import jax
import jax.numpy as jnp
import numpy as np
from jax import lax

NVAR = 5
BLOCK = 128
STEPS = 2
AXL = 4
SC = 8
RB_DEV = 8
PAIRS_DEV = 32
COEF = 160
CAP = 2
SPANC = 64
PITCH = 4096
RBLK = 256
PAIRS = 1024
N_ROWS = 32
N_SPAN = 8


def touch_ends(array, key, low, top_value):
    place = [jax.random.randint(jax.random.fold_in(key, axis), (), 0, length) for axis, length in enumerate(array.shape)]
    longest = array.shape.index(max(array.shape))
    beside = place[:longest] + [(place[longest] + 1) % array.shape[longest]] + place[longest + 1:]
    return array.at[tuple(place)].set(low).at[tuple(beside)].set(top_value)


def steps_of(stream_key, dims, cuts, smallest, largest):
    factor_of = 1.0
    for axis_at, shards_of in cuts:
        steps = jax.random.uniform(jax.random.fold_in(jax.random.fold_in(stream_key, 6), axis_at), (shards_of,), jnp.float32, smallest / len(cuts), largest / len(cuts))
        factor_of = factor_of * jnp.repeat(jnp.exp(steps), dims[axis_at] // shards_of).reshape((-1,) + (1,) * (len(dims) - 1 - axis_at))
    return factor_of


def assign_block(rng, own, number, rows, number_of, top, bound, lean):
    ranking = jax.random.permutation(rng, number_of)
    packed, ordinary = portions_of(number_of, rows * top, bound, lean, True), portions_of(number_of, rows * top, bound, lean, False)
    places = jnp.arange(number_of)

    def named(lengths, turn):
        used = int((lengths > 0).sum())
        fixed = max(1, used // 4)
        shifted = fixed + (places - fixed + turn * (used - fixed)) % max(1, number_of - fixed)
        return jnp.zeros((number_of,), jnp.int32).at[ranking[jnp.where(places < fixed, places, shifted)]].set(jnp.asarray(lengths, jnp.int32))

    lengths = jnp.where(number % 4 == 0, named(packed, number // 4), named(ordinary, number - number // 4 - 1))
    mixed = jax.random.permutation(jax.random.fold_in(own, 3), number_of)
    source_of, taker = mixed[0:number_of // 2 * 2:2], mixed[1:number_of // 2 * 2:2]
    room = jnp.minimum(lengths[source_of] - 1, bound - lengths[taker]) // 2
    room = jnp.where((source_of == ranking[0]) | (taker == ranking[0]) | (lengths[taker] == 0), 0, jnp.maximum(room, 0))
    shifted = jax.random.randint(jax.random.fold_in(own, 4), (number_of // 2,), 0, 1 << 20) % (room + 1)
    lengths = lengths.at[source_of].add(-shifted).at[taker].add(shifted)
    labels = jnp.searchsorted(jnp.cumsum(lengths), jnp.arange(rows * top), side="right").astype(jnp.int32)
    listing = labels.reshape(top, rows).T
    listing = listing[jax.random.permutation(jax.random.fold_in(own, 1), rows)]
    turn = jax.random.randint(jax.random.fold_in(own, 2), (rows, 1), 0, top)
    return jnp.take_along_axis(listing, (jnp.arange(top)[None, :] + turn) % top, axis=1)


def portions_of(amount, total, most, slope, full):
    portions = [(1 << 20) // math.isqrt(standing ** slope) + 1 for standing in range(1, amount + 1)]
    largest = most if full else min(most, max(-(-total // amount), total * portions[0] // sum(portions)))
    least = 1 if total - largest >= amount - 1 else 0
    holding, rest = [largest] + [least] * (amount - 1), total - largest - least * (amount - 1)
    while rest > 0:
        movable = [i for i in range(1, amount) if holding[i] < largest] or [i for i in range(1, amount) if holding[i] < most]
        mass, budget = sum([portions[i] for i in movable]), rest
        for i in movable:
            more = min(most - holding[i], max(1, budget * portions[i] // mass), rest)
            holding[i] = holding[i] + more
            rest = rest - more
    return np.array(holding)


def scatter_about(own_key, shape, spread, bound, cuts=(), held_as=jnp.bfloat16):
    result = spread * jax.random.normal(own_key, shape, jnp.float32)
    if cuts:
        result = result * steps_of(own_key, shape, cuts, -0.22, 0.18)
    return jnp.clip(result, -bound, bound).astype(held_as)


def setup_inputs(seed: int = 0) -> dict:
    seeds = jax.random.split(jax.random.key(seed), 8)
    rotor_face = scatter_about(seeds[0], (N_SPAN, RBLK, COEF, BLOCK), 1.0, 6.0, ((0, 8), (1, 32)))
    pair_source_keys = jax.random.split(jax.random.fold_in(seeds[1], 1), N_SPAN * PAIRS // PAIRS_DEV)
    pair_source_turns = jax.random.permutation(jax.random.fold_in(seeds[1], 3), N_SPAN * PAIRS // PAIRS_DEV)
    pair_source = jax.vmap(lambda own, number: assign_block(jax.random.fold_in(seeds[1], 2), own, number, PAIRS_DEV, N_ROWS, 1, CAP, 2))(pair_source_keys, pair_source_turns).reshape((N_SPAN, PAIRS, 1))
    pair_block = touch_ends(jax.random.randint(seeds[2], (N_SPAN, PAIRS), 0, RB_DEV), jax.random.fold_in(seeds[2], 1), 0, RB_DEV - 1).astype(jnp.int32)
    pair_row = touch_ends(jax.random.randint(seeds[3], (N_SPAN, PAIRS), 0, SC), jax.random.fold_in(seeds[3], 1), 0, SC - 1).astype(jnp.int32)
    pair_weight = scatter_about(seeds[4], (N_SPAN, PAIRS, BLOCK, BLOCK), BLOCK ** -0.5, 0.5, ((0, 8), (1, 32)))
    stator_field = scatter_about(seeds[5], (AXL, COEF, SPANC, PITCH), 1.0, 6.0, ((2, 8), (3, 32)), jnp.float32)
    damping = jnp.clip(jnp.exp(math.log(0.5) - 2.3025851 * jax.random.uniform(seeds[6], (SPANC, PITCH), jnp.float32) ** steps_of(seeds[6], (SPANC, PITCH), ((0, 8), (1, 32)), -0.2, 0.2)), 0.05, 0.5)
    return {"rotor_face": rotor_face, "pair_source": pair_source, "pair_block": pair_block, "pair_row": pair_row, "pair_weight": pair_weight, "stator_field": stator_field, "damping": damping}


UPWIND = 0.45
DIFFUSE = 0.2
TURNING = 0.02


def harmonic_turn(field, nvars):
    shape = field.shape
    split = field.reshape(shape[0], nvars, -1, 2, shape[2], shape[3])
    count = split.shape[2]
    order = (jnp.arange(count, dtype=jnp.float32) + 1.0).reshape(1, 1, count, 1, 1)
    real_part = split[:, :, :, 0]
    imag_part = split[:, :, :, 1]
    return jnp.stack([order * imag_part, -order * real_part], axis=3).reshape(shape)


def reference(rotor_face, pair_source, pair_block, pair_row, pair_weight, stator_field, damping):
    def one_receiver(index):
        band = index // N_ROWS
        device = index % N_ROWS
        first = (device * PAIRS_DEV).astype(jnp.int32)
        sources = lax.dynamic_slice_in_dim(pair_source[band][:, 0], first, PAIRS_DEV)
        blocks = lax.dynamic_slice_in_dim(pair_block[band], first, PAIRS_DEV)
        targets = lax.dynamic_slice_in_dim(pair_row[band], first, PAIRS_DEV)
        weights = lax.dynamic_slice_in_dim(pair_weight[band], first, PAIRS_DEV)
        chosen = jnp.take(rotor_face[band], (sources * RB_DEV + blocks).astype(jnp.int32), axis=0)
        terms = jnp.einsum("pck,pki->pci", chosen.astype(jnp.float32), weights.astype(jnp.float32), precision=lax.Precision.HIGHEST)
        hits = (targets[:, None] == jnp.arange(SC, dtype=jnp.int32)[None, :]).astype(jnp.float32)
        return jnp.einsum("pr,pci->cri", hits, terms, precision=lax.Precision.HIGHEST)

    faces = lax.map(one_receiver, jnp.arange(N_SPAN * N_ROWS, dtype=jnp.int32))
    faces = faces.reshape(N_SPAN, N_ROWS, COEF, SC, BLOCK)
    interface = jnp.transpose(faces, (2, 0, 3, 1, 4)).reshape(COEF, SPANC, PITCH)
    field = stator_field
    for section in range(STEPS):
        padded = jnp.pad(field, ((0, 0), (0, 0), (1, 1), (0, 0)))
        beside = padded[:, :, 2:, :] + padded[:, :, :-2, :] + jnp.roll(field, -1, axis=3) + jnp.roll(field, 1, axis=3)
        upstream = jnp.concatenate([interface[None], field[:-1]], axis=0)
        field = field + UPWIND * (upstream - field) + DIFFUSE * (beside - 4.0 * field) - damping * field + TURNING * harmonic_turn(field, NVAR)
    return interface, field
```

```python
import functools

import jax
import jax.numpy as jnp
from jax import lax
from jax.experimental import pallas as pl
from jax.experimental.pallas import tpu as pltpu
from jax.sharding import PartitionSpec as P

NVAR = 5
UPWIND = 0.45
DIFFUSE = 0.2
TURNING = 0.02
NY = 4
NZ = 8
CAP = 2
GROUP = 32
VMEM = pl.BlockSpec(memory_space=pltpu.VMEM)
SMEM = pl.BlockSpec(memory_space=pltpu.SMEM)
STAGES = ((0, -1, 1, -2, 2, -3, 3, 4),)


def rows8(start):
    return pl.ds(pl.multiple_of(start, 8), 8)


def pack_edges(tiles, lane4):
    packed = jnp.zeros((8, 128), jnp.float32)
    for c, tile in enumerate(tiles):
        packed = jnp.where(lane4 == c, pltpu.roll(tile, 4 * c + 1, 1), packed)
    return packed


def edges_kernel(v_ref, packed_ref, top_ref, bottom_ref):
    coefs = top_ref.shape[0]
    lane4 = lax.broadcasted_iota(jnp.int32, (8, 128), 1) // 4
    top_ref[...] = v_ref[pl.ds(0, coefs, stride=8), :]
    bottom_ref[...] = v_ref[pl.ds(7, coefs, stride=8), :]

    def body(i, carry):
        base = i * (GROUP * 8)
        tiles = [v_ref[rows8(base + 8 * c), :] for c in range(GROUP)]
        packed_ref[i] = pack_edges(tiles, lane4)
        return carry

    lax.fori_loop(0, coefs // GROUP, body, 0)


def combine_halo(left, right, lane):
    return jnp.where(lane % 4 == 1, pltpu.roll(left, 1, 1), pltpu.roll(right, 127, 1))


def operator_pair(x0, x1, s0, s1, h, c, k, diag, row, lane):
    out = []
    for j, (x, s) in enumerate(((x0, s0), (x1, s1))):
        edge = pltpu.roll(h, (128 - (4 * (c + j) + 1)) % 128, 1)
        above = jnp.where(row == 0, s, pltpu.roll(x, 1, 0))
        below = jnp.where(row == 7, s, pltpu.roll(x, 7, 0))
        left = jnp.where(lane == 0, edge, pltpu.roll(x, 1, 1))
        right = jnp.where(lane == 127, edge, pltpu.roll(x, 127, 1))
        beside = (above + below) + (left + right)
        turn = (TURNING * k) * x1 if j == 0 else (-TURNING * k) * x0
        out.append(diag * x + DIFFUSE * beside + turn)
    return out


def section_kernel(with_edges, v_ref, top_ref, bottom_ref, left_ref, right_ref, damp_ref, out_ref, *rest):
    if with_edges:
        packed_ref, new_top_ref, new_bottom_ref, halo = rest
    else:
        (halo,) = rest
    coefs = top_ref.shape[0]
    groups = coefs // GROUP
    row = lax.broadcasted_iota(jnp.int32, (8, 128), 0)
    lane = lax.broadcasted_iota(jnp.int32, (8, 128), 1)
    halo[pl.ds(0, coefs, stride=8), :] = top_ref[...]
    halo[pl.ds(7, coefs, stride=8), :] = bottom_ref[...]
    diag = (1.0 - UPWIND - 4.0 * DIFFUSE) - damp_ref[...]

    def body(i, carry):
        base = i * (GROUP * 8)
        behind = jnp.maximum(i - NVAR, 0) * (GROUP * 8)
        upwind = jnp.where(i >= NVAR, UPWIND, 0.0).astype(jnp.float32)
        h = combine_halo(left_ref[i], right_ref[i], lane)
        packed = jnp.zeros((8, 128), jnp.float32)
        for c in range(0, GROUP, 2):
            at = [rows8(base + 8 * (c + j)) for j in range(2)]
            new = operator_pair(
                v_ref[at[0], :], v_ref[at[1], :], halo[at[0], :], halo[at[1], :],
                h, c, float(c // 2 + 1), diag, row, lane,
            )
            for j in range(2):
                tile = new[j] + upwind * v_ref[rows8(behind + 8 * (c + j)), :]
                out_ref[at[j], :] = tile
                if with_edges:
                    packed = jnp.where(lane // 4 == c + j, pltpu.roll(tile, 4 * (c + j) + 1, 1), packed)
        if with_edges:
            packed_ref[i] = packed
        return carry

    lax.fori_loop(0, groups, body, 0)
    if with_edges:
        new_top_ref[...] = out_ref[pl.ds(0, coefs, stride=8), :]
        new_bottom_ref[...] = out_ref[pl.ds(7, coefs, stride=8), :]


def finish_kernel(face_ref, top_ref, bottom_ref, left_ref, right_ref, damp_ref, part_ref, out_ref, halo):
    coefs = top_ref.shape[0]
    row = lax.broadcasted_iota(jnp.int32, (8, 128), 0)
    lane = lax.broadcasted_iota(jnp.int32, (8, 128), 1)
    halo[pl.ds(0, coefs, stride=8), :] = top_ref[...]
    halo[pl.ds(7, coefs, stride=8), :] = bottom_ref[...]
    diag = (2.0 - UPWIND - 4.0 * DIFFUSE) - damp_ref[...]

    def body(i, carry):
        base = i * (GROUP * 8)
        h = combine_halo(left_ref[i], right_ref[i], lane)
        for c in range(0, GROUP, 2):
            at = [rows8(base + 8 * (c + j)) for j in range(2)]
            x = [face_ref[a, :] for a in at]
            new = operator_pair(
                x[0], x[1], halo[at[0], :], halo[at[1], :], h, c, float(c // 2 + 1), diag, row, lane
            )
            for j in range(2):
                out_ref[at[j], :] = part_ref[at[j], :] + UPWIND * new[j]
                nxt = rows8(coefs * 8 + base + 8 * (c + j))
                out_ref[nxt, :] = part_ref[nxt, :] + (UPWIND * UPWIND) * x[j]
        return carry

    lax.fori_loop(0, coefs // GROUP, body, 0)


def plan_kernel(where_ref, own_ref, near_ref, far_ref, back_ref, send_ref, slot_ref, count):
    my_z = where_ref[0]
    my_y = where_ref[1]

    def clear(i, carry):
        send_ref[i] = 0
        return carry

    lax.fori_loop(0, NY * NZ * CAP, clear, 0)
    for shift, asked in enumerate((own_ref, near_ref, far_ref, back_ref)):
        peer = (my_y + shift) % NY

        def zero(i, carry):
            count[i] = 0
            return carry

        lax.fori_loop(0, NZ * NY, zero, 0)

        def pair(p, carry, asked=asked, peer=peer, shift=shift):
            source = asked[0, p]
            rank = jnp.minimum(count[source], CAP - 1)
            count[source] = rank + 1
            distance = (source // NY - my_z + NZ) % NZ

            @pl.when(source % NY == my_y)
            def _():
                send_ref[(peer * NZ + distance) * CAP + rank] = asked[1, p]

            if shift == 0:
                slot_ref[p] = ((source % NY) * NZ + distance) * CAP + rank
            return carry

        lax.fori_loop(0, asked.shape[1], pair, 0)


def select_kernel(stage, send_ref, *refs):
    out_ref = refs[-1]
    half = refs[0].shape[1]
    for peer in range(NY):
        for i, distance in enumerate(stage):
            for rank in range(CAP):
                block = send_ref[(peer * NZ + distance % NZ) * CAP + rank]
                slot = (peer * len(stage) + i) * CAP + rank
                out_ref[slot, :half] = refs[2 * i][block]
                out_ref[slot, half:] = refs[2 * i + 1][block]


def face_kernel(stage, slot_ref, row_ref, came_ref, weight_ref, face_ref, packed_ref, top_ref, bottom_ref, total):
    coefs = top_ref.shape[0]
    lane4 = lax.broadcasted_iota(jnp.int32, (8, 128), 1) // 4
    total[...] = jnp.zeros_like(total)
    place = {d % NZ: i for i, d in enumerate(stage)}
    for p in range(weight_ref.shape[0]):
        slot = slot_ref[p]
        distance = (slot // CAP) % NZ
        spot = jnp.int32(0)
        for d, i in place.items():
            spot = jnp.where(distance == d, i, spot)
        at = ((slot // (CAP * NZ)) * len(stage) + spot) * CAP + slot % CAP
        term = jnp.dot(came_ref[at], weight_ref[p], preferred_element_type=jnp.float32)
        total[row_ref[p]] += term
    for r in range(8):
        face_ref[pl.ds(r, coefs, stride=8), :] = total[r]
    top_ref[...] = total[0]
    bottom_ref[...] = total[7]

    def body(i, carry):
        tiles = [face_ref[rows8(i * (GROUP * 8) + 8 * c), :] for c in range(GROUP)]
        packed_ref[i] = pack_edges(tiles, lane4)
        return carry

    lax.fori_loop(0, coefs // GROUP, body, 0)


def f32(*shape):
    return jax.ShapeDtypeStruct(shape, jnp.float32)


def per_device(rotor_face, pair_source, pair_block, pair_row, pair_weight, stator_field, damping):
    coefs, width = rotor_face.shape[2:]
    layers = stator_field.shape[0]
    pairs = pair_block.shape[1]
    every = layers * coefs
    groups = every // GROUP
    n_span = lax.axis_size("span")
    n_rows = lax.axis_size("rows")
    me = lax.axis_index("rows")
    where = jnp.stack([me // NY, me % NY])

    def up_z(k):
        return [(i, (i // NY + k) % NZ * NY + i % NY) for i in range(n_rows)]

    def up_y(k):
        return [(i, i // NY * NY + (i % NY + k) % NY) for i in range(n_rows)]

    def halos(packed, top, bottom):
        left = lax.ppermute(packed, "rows", [(i, (i + 1) % n_rows) for i in range(n_rows)])
        right = lax.ppermute(packed, "rows", [((i + 1) % n_rows, i) for i in range(n_rows)])
        above = lax.ppermute(bottom, "span", [(i, i + 1) for i in range(n_span - 1)])
        below = lax.ppermute(top, "span", [(i + 1, i) for i in range(n_span - 1)])
        return above, below, left, right

    wanted = jnp.stack([pair_source[0, :, 0], pair_block[0]])
    asked = [wanted] + [lax.ppermute(wanted, "rows", up_y(-k)) for k in range(1, NY)]
    half = coefs // 2
    own = rotor_face[0]
    held = {0: [own[:, :half], own[:, half:]]}
    for k in range(1, NZ // 2):
        held[-k] = [lax.ppermute(held[1 - k][j], "rows", up_z(1)) for j in range(2)]
        held[k] = [lax.ppermute(held[k - 1][j], "rows", up_z(-1)) for j in range(2)]
    last = NZ // 2 - 1
    held[NZ // 2] = [
        lax.ppermute(held[-last][0], "rows", up_z(1)),
        lax.ppermute(held[last][1], "rows", up_z(-1)),
    ]

    send_table, slot_of = pl.pallas_call(
        plan_kernel,
        out_shape=(
            jax.ShapeDtypeStruct((NY * NZ * CAP,), jnp.int32),
            jax.ShapeDtypeStruct((pairs,), jnp.int32),
        ),
        in_specs=[SMEM] * 5,
        out_specs=(SMEM, SMEM),
        scratch_shapes=[pltpu.SMEM((NZ * NY,), jnp.int32)],
        name="plan",
    )(where, *asked)

    flat = stator_field.reshape(every * 8, width)
    packed, top, bottom = pl.pallas_call(
        edges_kernel,
        out_shape=(f32(groups, 8, 128), f32(every, width), f32(every, width)),
        in_specs=[VMEM],
        out_specs=(VMEM,) * 3,
        name="edges",
    )(flat)
    first, packed, top, bottom = pl.pallas_call(
        functools.partial(section_kernel, True),
        out_shape=(f32(every * 8, width), f32(groups, 8, 128), f32(every, width), f32(every, width)),
        in_specs=[VMEM] * 6,
        out_specs=(VMEM,) * 4,
        scratch_shapes=[pltpu.VMEM((every * 8, width), jnp.float32)],
        name="section_one",
    )(flat, *halos(packed, top, bottom), damping)
    second = pl.pallas_call(
        functools.partial(section_kernel, False),
        out_shape=f32(every * 8, width),
        in_specs=[VMEM] * 6,
        out_specs=VMEM,
        scratch_shapes=[pltpu.VMEM((every * 8, width), jnp.float32)],
        name="section_two",
    )(first, *halos(packed, top, bottom), damping)

    stage = STAGES[0]
    slots = NY * len(stage) * CAP
    sent = pl.pallas_call(
        functools.partial(select_kernel, stage),
        out_shape=jax.ShapeDtypeStruct((slots, coefs, width), jnp.bfloat16),
        in_specs=[SMEM] + [VMEM] * (2 * len(stage)),
        out_specs=VMEM,
        name="select",
    )(send_table, *(held[d][j] for d in stage for j in range(2)))
    same_z = [[z * NY + y for y in range(NY)] for z in range(NZ)]
    came = lax.all_to_all(sent, "rows", split_axis=0, concat_axis=0, tiled=True, axis_index_groups=same_z)
    face, packed, top, bottom = pl.pallas_call(
        functools.partial(face_kernel, stage),
        out_shape=(f32(coefs * 8, width), f32(coefs // GROUP, 8, 128), f32(coefs, width), f32(coefs, width)),
        in_specs=[SMEM, SMEM, VMEM, VMEM],
        out_specs=(VMEM,) * 4,
        scratch_shapes=[pltpu.VMEM((8, coefs, width), jnp.float32)],
        name="face",
    )(slot_of, pair_row[0], came, pair_weight[0])

    two = pl.BlockSpec((2 * coefs * 8, width), lambda i: (0, 0))
    updated = pl.pallas_call(
        finish_kernel,
        grid=(1,),
        out_shape=f32(every * 8, width),
        in_specs=[VMEM] * 6 + [two],
        out_specs=two,
        scratch_shapes=[pltpu.VMEM((coefs * 8, width), jnp.float32)],
        input_output_aliases={6: 0},
        name="finish",
    )(face, *halos(packed, top, bottom), damping, second)
    return face.reshape(coefs, 8, width), updated.reshape(stator_field.shape)


def solution(mesh):
    placed = (
        P("span", "rows", None, None),
        P("span", "rows", None),
        P("span", "rows"),
        P("span", "rows"),
        P("span", "rows", None, None),
        P(None, None, "span", "rows"),
        P("span", "rows"),
    )
    return jax.shard_map(
        per_device,
        mesh=mesh,
        in_specs=placed,
        out_specs=(P(None, "span", "rows"), P(None, None, "span", "rows")),
        check_vma=False,
    )
```

```python
import functools

import jax
import jax.numpy as jnp
from jax import lax
from jax.experimental import pallas as pl
from jax.experimental.pallas import tpu as pltpu
from jax.sharding import PartitionSpec as P

NVAR = 5
UPWIND = 0.45
DIFFUSE = 0.2
TURNING = 0.02
NY = 4
NZ = 8
CAP = 2
GROUP = 32
BATCH = 16
VMEM = pl.BlockSpec(memory_space=pltpu.VMEM)
SMEM = pl.BlockSpec(memory_space=pltpu.SMEM)
PARAMS = pltpu.CompilerParams(vmem_limit_bytes=24 << 20)
STAGES = ((0, -1, 1, -2, 2), (-3, 3, 4))


def rows8(start):
    return pl.ds(pl.multiple_of(start, 8), 8)


def lanes():
    return lax.broadcasted_iota(jnp.int32, (8, 128), 1)


def pack_edges(tiles, lane4):
    packed = jnp.zeros((8, 128), jnp.float32)
    for c, tile in enumerate(tiles):
        packed = jnp.where(lane4 == c, pltpu.roll(tile, 4 * c + 1, 1), packed)
    return packed


def edges_kernel(v_ref, packed_ref, top_ref, bottom_ref):
    coefs = top_ref.shape[0]
    lane4 = lanes() // 4
    for i in range(coefs // GROUP):
        packed_ref[i] = pack_edges([v_ref[rows8(8 * (GROUP * i + c)), :] for c in range(GROUP)], lane4)
    top_ref[...] = v_ref[pl.ds(0, coefs, stride=8), :]
    bottom_ref[...] = v_ref[pl.ds(7, coefs, stride=8), :]


def combine_halo(left, right, lane):
    return jnp.where(lane % 4 == 1, pltpu.roll(left, 1, 1), pltpu.roll(right, 127, 1))


def operator(xs, aboves, belows, h, first, diag, row, lane):
    out = []
    for j, x in enumerate(xs):
        c = first + j
        k = float(c // 2 + 1)
        edge = pltpu.roll(h, (128 - (4 * c + 1)) % 128, 1)
        above = jnp.where(row == 0, aboves[j], pltpu.roll(x, 1, 0))
        below = jnp.where(row == 7, belows[j], pltpu.roll(x, 7, 0))
        left = jnp.where(lane == 0, edge, pltpu.roll(x, 1, 1))
        right = jnp.where(lane == 127, edge, pltpu.roll(x, 127, 1))
        beside = (above + below) + (left + right)
        turn = (TURNING * k) * xs[j + 1] if j % 2 == 0 else (-TURNING * k) * xs[j - 1]
        out.append((diag * x + DIFFUSE * beside) + turn)
    return out


def section_kernel(with_edges, v_ref, behind_ref, top_ref, bottom_ref, left_ref, right_ref, damp_ref, out_ref, *rest):
    coefs = top_ref.shape[0]
    row = lax.broadcasted_iota(jnp.int32, (8, 128), 0)
    lane = lanes()
    diag = (1.0 - UPWIND - 4.0 * DIFFUSE) - damp_ref[...]
    upwind = UPWIND
    if with_edges:
        upwind = jnp.where(pl.program_id(0) > 0, UPWIND, 0.0).astype(jnp.float32)

    def body(i, carry):
        base = i * GROUP
        h = combine_halo(left_ref[i], right_ref[i], lane)
        packed = jnp.zeros((8, 128), jnp.float32)
        for first in range(0, GROUP, BATCH):
            at = [rows8(8 * (base + first + j)) for j in range(BATCH)]
            one = [pl.ds(base + first + j, 1) for j in range(BATCH)]
            new = operator(
                [v_ref[a, :] for a in at], [top_ref[o, :] for o in one], [bottom_ref[o, :] for o in one],
                h, first, diag, row, lane,
            )
            new = [n + upwind * behind_ref[a, :] for n, a in zip(new, at)]
            if with_edges:
                for j in range(BATCH):
                    c = first + j
                    packed = jnp.where(lane // 4 == c, pltpu.roll(new[j], 4 * c + 1, 1), packed)
            for j in range(BATCH):
                out_ref[at[j], :] = new[j]
        if with_edges:
            rest[0][i] = packed
        return carry

    lax.fori_loop(0, coefs // GROUP, body, 0)
    if with_edges:
        rest[1][...] = out_ref[pl.ds(0, coefs, stride=8), :]
        rest[2][...] = out_ref[pl.ds(7, coefs, stride=8), :]


def plan_kernel(where_ref, own_ref, near_ref, far_ref, back_ref, table_ref, slot_ref, stage_ref, first):
    my_z = where_ref[0]
    my_y = where_ref[1]
    n = NY * NZ
    pairs = slot_ref.shape[0]
    for i in range(CAP * NY * n):
        table_ref[i] = 0
    for shift, asked in enumerate((own_ref, near_ref, far_ref, back_ref)):
        base = lax.rem(my_y + shift, NY) * n
        for p in range(pairs):
            table_ref[NY * n + base + asked[0, p]] = asked[1, p]
        for p in reversed(range(pairs)):
            table_ref[base + asked[0, p]] = asked[1, p]
    for p in reversed(range(pairs)):
        first[own_ref[0, p]] = p
    for p in range(pairs):
        source = own_ref[0, p]
        rank = jnp.where(first[source] == p, 0, 1)
        distance = lax.rem(lax.div(source, NY) + (NZ - my_z), NZ)
        spot, size, at_stage = jnp.int32(0), jnp.int32(0), jnp.int32(0)
        for g, stage in enumerate(STAGES):
            for i, d in enumerate(stage):
                hit = distance == d % NZ
                spot = jnp.where(hit, i, spot)
                size = jnp.where(hit, len(stage), size)
                at_stage = jnp.where(hit, g, at_stage)
        slot_ref[p] = (lax.rem(source, NY) * size + spot) * CAP + rank
        stage_ref[p] = at_stage


def select_kernel(stage, where_ref, table_ref, *refs):
    out_ref, slots, sems = refs[-3:]
    my_z = where_ref[0]
    my_y = where_ref[1]
    n = NY * NZ
    each = len(stage) * CAP
    copies = []
    for peer in range(NY):
        for i, distance in enumerate(stage):
            source = lax.rem(my_z + (distance + NZ), NZ) * NY + my_y
            for rank in range(CAP):
                block = table_ref[(rank * NY + peer) * n + source]
                slot = peer * each + i * CAP + rank
                if distance == NZ // 2:
                    half = refs[i].shape[0]
                    low = refs[i][jnp.minimum(block, half - 1)]
                    high = refs[i + 1][jnp.maximum(block - half, 0)]
                    slots[slot] = jnp.where(block < half, low, high)
                else:
                    slots[slot] = refs[i][block]
        here = pl.ds(peer * each, each)
        copies.append(pltpu.make_async_copy(slots.at[here], out_ref.at[here], sems.at[peer]))
        copies[-1].start()
    for copy in copies:
        copy.wait()


def face_kernel(
    slot_ref, stage_ref, row_ref, came_ref, late_ref, weight_hbm, *refs
):
    face_ref, chain_ref, packed_ref, top_ref, bottom_ref = refs[4:9]
    total, blocks, weight_ref, layer, packed, top, bottom, block_sems, sems = refs[9:]
    coefs = top.shape[0]
    deep = coefs * 8
    pairs = row_ref.shape[0]
    weights = pltpu.make_async_copy(weight_hbm, weight_ref, sems.at[0])
    weights.start()
    for p in range(pairs):
        for g, ref in enumerate((came_ref, late_ref)):

            @pl.when(stage_ref[p] == g)
            def _(p=p, ref=ref):
                pltpu.make_async_copy(ref.at[slot_ref[p]], blocks.at[p], block_sems.at[p]).start()

    second = chain_ref.at[pl.ds(deep, deep)]
    part = pltpu.make_async_copy(second, layer, sems.at[1])
    part.start()
    total[...] = jnp.zeros_like(total)
    weights.wait()
    for p in range(pairs):
        pltpu.make_async_copy(came_ref.at[0], blocks.at[p], block_sems.at[p]).wait()
    part.wait()
    for p in range(pairs):
        total[row_ref[p]] += jnp.dot(blocks[p], weight_ref[p], preferred_element_type=jnp.float32)
    for r in range(8):
        face_ref[pl.ds(r, coefs, stride=8), :] = total[r]
    out = [pltpu.make_async_copy(face_ref, chain_ref.at[pl.ds(0, deep)], sems.at[2])]
    out[0].start()
    lane4 = lanes() // 4
    for i in range(coefs // GROUP):
        at = [rows8(8 * (GROUP * i + c)) for c in range(GROUP)]
        tiles = [layer[a, :] + UPWIND * face_ref[a, :] for a in at]
        packed[i] = pack_edges(tiles, lane4)
        for a, tile in zip(at, tiles):
            layer[a, :] = tile
    top[...] = layer[pl.ds(0, coefs, stride=8), :]
    bottom[...] = layer[pl.ds(7, coefs, stride=8), :]
    out += [
        pltpu.make_async_copy(layer, second, sems.at[3]),
        pltpu.make_async_copy(packed, packed_ref.at[pl.ds(0, coefs // GROUP)], sems.at[4]),
        pltpu.make_async_copy(top, top_ref.at[pl.ds(0, coefs)], sems.at[5]),
        pltpu.make_async_copy(bottom, bottom_ref.at[pl.ds(0, coefs)], sems.at[6]),
    ]
    for copy in out[1:]:
        copy.start()
    for copy in out:
        copy.wait()


def f32(*shape):
    return jax.ShapeDtypeStruct(shape, jnp.float32)


def per_device(rotor_face, pair_source, pair_block, pair_row, pair_weight, stator_field, damping):
    coefs, width = rotor_face.shape[2:]
    layers = stator_field.shape[0]
    pairs = pair_block.shape[1]
    every = layers * coefs
    deep = coefs * 8
    parts = coefs // GROUP
    n_span = lax.axis_size("span")
    n_rows = lax.axis_size("rows")
    me = lax.axis_index("rows")
    where = jnp.stack([me // NY, me % NY])
    barrier = lax.optimization_barrier

    def up_z(x, k):
        return lax.ppermute(x, "rows", [(i, (i // NY + k) % NZ * NY + i % NY) for i in range(n_rows)])

    def from_y(x, k):
        return lax.ppermute(x, "rows", [(i // NY * NY + (i % NY + k) % NY, i) for i in range(n_rows)])

    def halos(packed, top, bottom):
        left = lax.ppermute(packed, "rows", [(i, (i + 1) % n_rows) for i in range(n_rows)])
        right = lax.ppermute(packed, "rows", [((i + 1) % n_rows, i) for i in range(n_rows)])
        above = lax.ppermute(bottom, "span", [(i, i + 1) for i in range(n_span - 1)])
        below = lax.ppermute(top, "span", [(i + 1, i) for i in range(n_span - 1)])
        return above, below, left, right

    wanted = jnp.stack([pair_source[0, :, 0], pair_block[0]])
    own = rotor_face[0]
    up, down = up_z(own, 1), up_z(own, -1)
    asked = [wanted] + [from_y(wanted, k) for k in range(1, NY)]
    flat = stator_field.reshape(every * 8, width)

    def block(*shape):
        return pl.BlockSpec(shape, lambda i: (i,) + (0,) * (len(shape) - 1))

    tile = pl.BlockSpec((8, width), lambda i: (0, 0))
    edge_specs = (block(parts, 8, 128), block(coefs, width), block(coefs, width))
    edge_shapes = (f32(every // GROUP, 8, 128), f32(every, width), f32(every, width))
    edges = pl.pallas_call(
        edges_kernel,
        grid=(layers,),
        out_shape=edge_shapes,
        in_specs=[block(deep, width)],
        out_specs=edge_specs,
        compiler_params=PARAMS,
        name="edges",
    )(flat)
    up, down, asked = barrier((up, down, asked))
    held = {0: own, -1: up, 1: down}
    up, down = up_z(up, 1), up_z(down, -1)
    table, slot_of, stage_of = pl.pallas_call(
        plan_kernel,
        out_shape=tuple(jax.ShapeDtypeStruct((m,), jnp.int32) for m in (CAP * NY * NY * NZ, pairs, pairs)),
        in_specs=[SMEM] * 5,
        out_specs=(SMEM,) * 3,
        scratch_shapes=[pltpu.SMEM((NY * NZ,), jnp.int32)],
        compiler_params=PARAMS,
        name="plan",
    )(where, *asked)
    up, down, table, edges = barrier((up, down, table, edges))
    held[-2], held[2] = up, down

    def exchange(stage, blocks):
        slots = NY * len(stage) * CAP
        sent = pl.pallas_call(
            functools.partial(select_kernel, stage),
            out_shape=jax.ShapeDtypeStruct((slots, coefs, width), jnp.bfloat16),
            in_specs=[SMEM, SMEM] + [VMEM] * len(blocks),
            out_specs=pl.BlockSpec(memory_space=pltpu.HBM),
            scratch_shapes=[pltpu.VMEM((slots, coefs, width), jnp.bfloat16), pltpu.SemaphoreType.DMA((NY,))],
            compiler_params=PARAMS,
            name="select",
        )(where, table, *blocks)
        same_z = [[z * NY + y for y in range(NY)] for z in range(NZ)]
        return sent, lax.all_to_all(sent, "rows", split_axis=0, concat_axis=0, tiled=True, axis_index_groups=same_z)

    sent, came = exchange(STAGES[0], [held[d] for d in STAGES[0]])
    up, down = up_z(up, 1), up_z(down, -1)
    middle = own.shape[0] // 2
    up, down, edges = barrier((up, down, edges))
    held[-3], held[3] = up, down
    last = [up_z(up[:middle], 1), up_z(down[middle:], -1)]
    around = halos(*edges)
    sent, late = exchange(STAGES[1], [held[-3], held[3]] + last)

    flat, sent = barrier((flat, sent))

    def section(v, above, below, left, right, with_edges):
        def ahead(i):
            return (i + 1, 0)

        def here(i):
            return (i, 0)

        def back(i):
            return (jnp.maximum(i - 1, 0), 0)

        shape, maps = (every * 8, width), (ahead, here, here)
        if with_edges:
            shape, maps = (every * 8 + deep, width), (here, back, ahead)
        layer_specs = [pl.BlockSpec((deep, width), m) for m in maps]
        return pl.pallas_call(
            functools.partial(section_kernel, with_edges),
            grid=(layers,),
            out_shape=(f32(*shape),) + (edge_shapes if with_edges else ()),
            in_specs=layer_specs[:2] + [
                block(coefs, width), block(coefs, width), block(parts, 8, 128), block(parts, 8, 128), tile,
            ],
            out_specs=(layer_specs[2],) + (edge_specs if with_edges else ()),
            compiler_params=PARAMS,
            name="section_one" if with_edges else "section_two",
        )(v, v, above, below, left, right, damping)

    chain, packed, top, bottom = section(flat, *around, True)
    any_space = pl.BlockSpec(memory_space=pl.ANY)
    face, chain, packed, top, bottom = pl.pallas_call(
        face_kernel,
        out_shape=(f32(deep, width), f32(every * 8 + deep, width)) + edge_shapes,
        in_specs=[SMEM] * 3 + [any_space] * 7,
        out_specs=(VMEM,) + (any_space,) * 4,
        scratch_shapes=[
            pltpu.VMEM((8, coefs, width), jnp.float32),
            pltpu.VMEM((pairs, coefs, width), jnp.bfloat16),
            pltpu.VMEM((pairs, width, width), jnp.bfloat16),
            pltpu.VMEM((deep, width), jnp.float32),
            pltpu.VMEM((parts, 8, 128), jnp.float32),
            pltpu.VMEM((coefs, width), jnp.float32),
            pltpu.VMEM((coefs, width), jnp.float32),
            pltpu.SemaphoreType.DMA((pairs,)),
            pltpu.SemaphoreType.DMA((7,)),
        ],
        input_output_aliases={6: 1, 7: 2, 8: 3, 9: 4},
        compiler_params=pltpu.CompilerParams(vmem_limit_bytes=52 << 20),
        name="face",
    )(slot_of, stage_of, pair_row[0], came, late, pair_weight[0], chain, packed, top, bottom)
    (updated,) = section(chain, *halos(packed, top, bottom), False)
    return face.reshape(coefs, 8, width), updated.reshape(stator_field.shape)


def solution(mesh):
    placed = (
        P("span", "rows", None, None),
        P("span", "rows", None),
        P("span", "rows"),
        P("span", "rows"),
        P("span", "rows", None, None),
        P(None, None, "span", "rows"),
        P("span", "rows"),
    )
    return jax.shard_map(
        per_device,
        mesh=mesh,
        in_specs=placed,
        out_specs=(P(None, "span", "rows"), P(None, None, "span", "rows")),
        check_vma=False,
    )
```

```python
import functools

import jax
import jax.numpy as jnp
from jax import lax
from jax.experimental import pallas as pl
from jax.experimental.pallas import tpu as pltpu
from jax.sharding import PartitionSpec as P


UPWIND = 0.45
DIFFUSE = 0.2
TURNING = 0.02
NY = 4
NZ = 8
CAP = 2
GROUP = 32
BATCH = 16
VMEM = pl.BlockSpec(memory_space=pltpu.VMEM)
SMEM = pl.BlockSpec(memory_space=pltpu.SMEM)
PARAMS = pltpu.CompilerParams(vmem_limit_bytes=24 << 20)
STAGES = ((0, -1, 1, -2, 2), (-3, 3, 4))


def rows8(start):
    return pl.ds(pl.multiple_of(start, 8), 8)


def lanes():
    return lax.broadcasted_iota(jnp.int32, (8, 128), 1)


def pack_edges(tiles, lane4):
    packed = jnp.zeros((8, 128), jnp.float32)
    for c, tile in enumerate(tiles):
        packed = jnp.where(lane4 == c, pltpu.roll(tile, 4 * c + 1, 1), packed)
    return packed


def edges_kernel(v_ref, packed_ref, top_ref, bottom_ref):
    coefs = top_ref.shape[0]
    lane4 = lanes() // 4
    for i in range(coefs // GROUP):
        packed_ref[i] = pack_edges([v_ref[rows8(8 * (GROUP * i + c)), :] for c in range(GROUP)], lane4)
    top_ref[...] = v_ref[pl.ds(0, coefs, stride=8), :]
    bottom_ref[...] = v_ref[pl.ds(7, coefs, stride=8), :]


def combine_halo(left, right, lane):
    return jnp.where(lane % 4 == 1, pltpu.roll(left, 1, 1), pltpu.roll(right, 127, 1))


def operator(xs, aboves, belows, h, first, diag, row, lane):
    out = []
    for j, x in enumerate(xs):
        c = first + j
        k = float(c // 2 + 1)
        edge = pltpu.roll(h, (128 - (4 * c + 1)) % 128, 1)
        above = jnp.where(row == 0, aboves[j], pltpu.roll(x, 1, 0))
        below = jnp.where(row == 7, belows[j], pltpu.roll(x, 7, 0))
        left = jnp.where(lane == 0, edge, pltpu.roll(x, 1, 1))
        right = jnp.where(lane == 127, edge, pltpu.roll(x, 127, 1))
        beside = (above + below) + (left + right)
        turn = (TURNING * k) * xs[j + 1] if j % 2 == 0 else (-TURNING * k) * xs[j - 1]
        out.append((diag * x + DIFFUSE * beside) + turn)
    return out


def section_kernel(with_edges, v_ref, behind_ref, top_ref, bottom_ref, left_ref, right_ref, damp_ref, out_ref, *rest):
    coefs = top_ref.shape[0]
    row = lax.broadcasted_iota(jnp.int32, (8, 128), 0)
    lane = lanes()
    diag = (1.0 - UPWIND - 4.0 * DIFFUSE) - damp_ref[...]
    upwind = UPWIND
    if with_edges:
        upwind = jnp.where(pl.program_id(0) > 0, UPWIND, 0.0).astype(jnp.float32)

    def body(i, carry):
        base = i * GROUP
        h = combine_halo(left_ref[i], right_ref[i], lane)
        packed = jnp.zeros((8, 128), jnp.float32)
        for first in range(0, GROUP, BATCH):
            at = [rows8(8 * (base + first + j)) for j in range(BATCH)]
            one = [pl.ds(base + first + j, 1) for j in range(BATCH)]
            new = operator(
                [v_ref[a, :] for a in at], [top_ref[o, :] for o in one], [bottom_ref[o, :] for o in one],
                h, first, diag, row, lane,
            )
            new = [n + upwind * behind_ref[a, :] for n, a in zip(new, at)]
            if with_edges:
                for j in range(BATCH):
                    c = first + j
                    packed = jnp.where(lane // 4 == c, pltpu.roll(new[j], 4 * c + 1, 1), packed)
            for j in range(BATCH):
                out_ref[at[j], :] = new[j]
        if with_edges:
            rest[0][i] = packed
        return carry

    lax.fori_loop(0, coefs // GROUP, body, 0)
    if with_edges:
        rest[1][...] = out_ref[pl.ds(0, coefs, stride=8), :]
        rest[2][...] = out_ref[pl.ds(7, coefs, stride=8), :]


def plan_kernel(where_ref, own_ref, near_ref, far_ref, back_ref, table_ref, slot_ref, stage_ref, first):
    my_z = where_ref[0]
    my_y = where_ref[1]
    n = NY * NZ
    pairs = slot_ref.shape[0]
    for i in range(CAP * NY * n):
        table_ref[i] = 0
    for shift, asked in enumerate((own_ref, near_ref, far_ref, back_ref)):
        base = lax.rem(my_y + shift, NY) * n
        for p in range(pairs):
            table_ref[NY * n + base + asked[0, p]] = asked[1, p]
        for p in reversed(range(pairs)):
            table_ref[base + asked[0, p]] = asked[1, p]
    for p in reversed(range(pairs)):
        first[own_ref[0, p]] = p
    for p in range(pairs):
        source = own_ref[0, p]
        rank = jnp.where(first[source] == p, 0, 1)
        distance = lax.rem(lax.div(source, NY) + (NZ - my_z), NZ)
        spot, size, at_stage = jnp.int32(0), jnp.int32(0), jnp.int32(0)
        for g, stage in enumerate(STAGES):
            for i, d in enumerate(stage):
                hit = distance == d % NZ
                spot = jnp.where(hit, i, spot)
                size = jnp.where(hit, len(stage), size)
                at_stage = jnp.where(hit, g, at_stage)
        slot_ref[p] = (lax.rem(source, NY) * size + spot) * CAP + rank
        stage_ref[p] = at_stage


def select_kernel(stage, where_ref, table_ref, *refs):
    out_ref, slots, sems = refs[-3:]
    my_z = where_ref[0]
    my_y = where_ref[1]
    n = NY * NZ
    each = len(stage) * CAP
    copies = []
    for peer in range(NY):
        for i, distance in enumerate(stage):
            source = lax.rem(my_z + (distance + NZ), NZ) * NY + my_y
            for rank in range(CAP):
                block = table_ref[(rank * NY + peer) * n + source]
                slot = peer * each + i * CAP + rank
                if distance == NZ // 2:
                    half = refs[i].shape[0]
                    low = refs[i][jnp.minimum(block, half - 1)]
                    high = refs[i + 1][jnp.maximum(block - half, 0)]
                    slots[slot] = jnp.where(block < half, low, high)
                else:
                    slots[slot] = refs[i][block]
        here = pl.ds(peer * each, each)
        copies.append(pltpu.make_async_copy(slots.at[here], out_ref.at[here], sems.at[peer]))
        copies[-1].start()
    for copy in copies:
        copy.wait()


def add_terms(stage, slot_ref, stage_ref, row_ref, came_ref, weight_ref, total, blocks, weights, block_sems, weight_sems):
    pairs = row_ref.shape[0]

    def copies(p, slot):
        yield pltpu.make_async_copy(came_ref.at[slot], blocks.at[p], block_sems.at[p])
        yield pltpu.make_async_copy(weight_ref.at[p], weights.at[p], weight_sems.at[p])

    for p in range(pairs):

        @pl.when(stage_ref[p] == stage)
        def _(p=p):
            for copy in copies(p, slot_ref[p]):
                copy.start()

    yield
    for p in range(pairs):

        @pl.when(stage_ref[p] == stage)
        def _(p=p):
            for copy in copies(p, 0):
                copy.wait()

    for p in range(pairs):
        term = jnp.dot(blocks[p], weights[p], preferred_element_type=jnp.float32)
        total[row_ref[p]] += jnp.where(stage_ref[p] == stage, term, 0.0)


def terms_kernel(stage, slot_ref, stage_ref, row_ref, came_ref, weight_ref, total, *scratch):
    work = add_terms(stage, slot_ref, stage_ref, row_ref, came_ref, weight_ref, total, *scratch)
    next(work)
    total[...] = jnp.zeros_like(total)
    next(work, None)


def face_kernel(stage, slot_ref, stage_ref, row_ref, came_ref, weight_ref, early_ref, *refs):
    face_ref, chain_ref, packed_ref, top_ref, bottom_ref = refs[4:9]
    total, layer, packed, top, bottom, sems = refs[9:15]
    coefs = top.shape[0]
    deep = coefs * 8
    work = add_terms(stage, slot_ref, stage_ref, row_ref, came_ref, weight_ref, total, *refs[15:])
    next(work)
    second = chain_ref.at[pl.ds(deep, deep)]
    part = pltpu.make_async_copy(second, layer, sems.at[1])
    part.start()
    total[...] = early_ref[...]
    next(work, None)
    part.wait()
    for r in range(8):
        face_ref[pl.ds(r, coefs, stride=8), :] = total[r]
    out = [pltpu.make_async_copy(face_ref, chain_ref.at[pl.ds(0, deep)], sems.at[2])]
    out[0].start()
    lane4 = lanes() // 4
    for i in range(coefs // GROUP):
        at = [rows8(8 * (GROUP * i + c)) for c in range(GROUP)]
        tiles = [layer[a, :] + UPWIND * face_ref[a, :] for a in at]
        packed[i] = pack_edges(tiles, lane4)
        for a, tile in zip(at, tiles):
            layer[a, :] = tile
    top[...] = layer[pl.ds(0, coefs, stride=8), :]
    bottom[...] = layer[pl.ds(7, coefs, stride=8), :]
    out += [
        pltpu.make_async_copy(layer, second, sems.at[3]),
        pltpu.make_async_copy(packed, packed_ref.at[pl.ds(0, coefs // GROUP)], sems.at[4]),
        pltpu.make_async_copy(top, top_ref.at[pl.ds(0, coefs)], sems.at[5]),
        pltpu.make_async_copy(bottom, bottom_ref.at[pl.ds(0, coefs)], sems.at[6]),
    ]
    for copy in out[1:]:
        copy.start()
    for copy in out:
        copy.wait()


def f32(*shape):
    return jax.ShapeDtypeStruct(shape, jnp.float32)


def per_device(rotor_face, pair_source, pair_block, pair_row, pair_weight, stator_field, damping):
    coefs, width = rotor_face.shape[2:]
    layers = stator_field.shape[0]
    pairs = pair_block.shape[1]
    every = layers * coefs
    deep = coefs * 8
    parts = coefs // GROUP
    n_span = lax.axis_size("span")
    n_rows = lax.axis_size("rows")
    me = lax.axis_index("rows")
    where = jnp.stack([me // NY, me % NY])
    barrier = lax.optimization_barrier

    def up_z(x, k):
        return lax.ppermute(x, "rows", [(i, (i // NY + k) % NZ * NY + i % NY) for i in range(n_rows)])

    def from_y(x, k):
        return lax.ppermute(x, "rows", [(i // NY * NY + (i % NY + k) % NY, i) for i in range(n_rows)])

    def halos(packed, top, bottom):
        left = lax.ppermute(packed, "rows", [(i, (i + 1) % n_rows) for i in range(n_rows)])
        right = lax.ppermute(packed, "rows", [((i + 1) % n_rows, i) for i in range(n_rows)])
        above = lax.ppermute(bottom, "span", [(i, i + 1) for i in range(n_span - 1)])
        below = lax.ppermute(top, "span", [(i + 1, i) for i in range(n_span - 1)])
        return above, below, left, right

    wanted = jnp.stack([pair_source[0, :, 0], pair_block[0]])
    own = rotor_face[0]
    up, down = up_z(own, 1), up_z(own, -1)
    asked = [wanted] + [from_y(wanted, k) for k in range(1, NY)]
    flat = stator_field.reshape(every * 8, width)

    def block(*shape):
        return pl.BlockSpec(shape, lambda i: (i,) + (0,) * (len(shape) - 1))

    tile = pl.BlockSpec((8, width), lambda i: (0, 0))
    edge_specs = (block(parts, 8, 128), block(coefs, width), block(coefs, width))
    edge_shapes = (f32(every // GROUP, 8, 128), f32(every, width), f32(every, width))
    edges = pl.pallas_call(
        edges_kernel,
        grid=(layers,),
        out_shape=edge_shapes,
        in_specs=[block(deep, width)],
        out_specs=edge_specs,
        compiler_params=PARAMS,
        name="edges",
    )(flat)
    up, down, asked = barrier((up, down, asked))
    held = {0: own, -1: up, 1: down}
    up, down = up_z(up, 1), up_z(down, -1)
    table, slot_of, stage_of = pl.pallas_call(
        plan_kernel,
        out_shape=tuple(jax.ShapeDtypeStruct((m,), jnp.int32) for m in (CAP * NY * NY * NZ, pairs, pairs)),
        in_specs=[SMEM] * 5,
        out_specs=(SMEM,) * 3,
        scratch_shapes=[pltpu.SMEM((NY * NZ,), jnp.int32)],
        compiler_params=PARAMS,
        name="plan",
    )(where, *asked)
    up, down, table, edges = barrier((up, down, table, edges))
    held[-2], held[2] = up, down

    def exchange(stage, blocks):
        slots = NY * len(stage) * CAP
        sent = pl.pallas_call(
            functools.partial(select_kernel, stage),
            out_shape=jax.ShapeDtypeStruct((slots, coefs, width), jnp.bfloat16),
            in_specs=[SMEM, SMEM] + [VMEM] * len(blocks),
            out_specs=pl.BlockSpec(memory_space=pltpu.HBM),
            scratch_shapes=[pltpu.VMEM((slots, coefs, width), jnp.bfloat16), pltpu.SemaphoreType.DMA((NY,))],
            compiler_params=PARAMS,
            name="select",
        )(where, table, *blocks)
        same_z = [[z * NY + y for y in range(NY)] for z in range(NZ)]
        return sent, lax.all_to_all(sent, "rows", split_axis=0, concat_axis=0, tiled=True, axis_index_groups=same_z)

    sent, came = exchange(STAGES[0], [held[d] for d in STAGES[0]])
    up, down = up_z(up, 1), up_z(down, -1)
    middle = own.shape[0] // 2
    held[-3], held[3] = up, down
    last = [up_z(up[:middle], 1), up_z(down[middle:], -1)]
    around = halos(*edges)
    sent, late = exchange(STAGES[1], [held[-3], held[3]] + last)

    flat, sent = barrier((flat, sent))

    def section(v, above, below, left, right, with_edges):
        def ahead(i):
            return (i + 1, 0)

        def here(i):
            return (i, 0)

        def back(i):
            return (jnp.maximum(i - 1, 0), 0)

        shape, maps = (every * 8, width), (ahead, here, here)
        if with_edges:
            shape, maps = (every * 8 + deep, width), (here, back, ahead)
        layer_specs = [pl.BlockSpec((deep, width), m) for m in maps]
        return pl.pallas_call(
            functools.partial(section_kernel, with_edges),
            grid=(layers,),
            out_shape=(f32(*shape),) + (edge_shapes if with_edges else ()),
            in_specs=layer_specs[:2] + [
                block(coefs, width), block(coefs, width), block(parts, 8, 128), block(parts, 8, 128), tile,
            ],
            out_specs=(layer_specs[2],) + (edge_specs if with_edges else ()),
            compiler_params=PARAMS,
            name="section_one" if with_edges else "section_two",
        )(v, v, above, below, left, right, damping)

    chain, packed, top, bottom = section(flat, *around, True)
    any_space = pl.BlockSpec(memory_space=pl.ANY)
    move = [
        pltpu.VMEM((pairs, coefs, width), jnp.bfloat16),
        pltpu.VMEM((pairs, width, width), jnp.bfloat16),
        pltpu.SemaphoreType.DMA((pairs,)),
        pltpu.SemaphoreType.DMA((pairs,)),
    ]
    early = pl.pallas_call(
        functools.partial(terms_kernel, 0),
        out_shape=f32(8, coefs, width),
        in_specs=[SMEM] * 3 + [any_space] * 2,
        out_specs=VMEM,
        scratch_shapes=move,
        compiler_params=PARAMS,
        name="terms",
    )(slot_of, stage_of, pair_row[0], came, pair_weight[0])
    face, chain, packed, top, bottom = pl.pallas_call(
        functools.partial(face_kernel, 1),
        out_shape=(f32(deep, width), f32(every * 8 + deep, width)) + edge_shapes,
        in_specs=[SMEM] * 3 + [any_space] * 2 + [VMEM] + [any_space] * 4,
        out_specs=(VMEM,) + (any_space,) * 4,
        scratch_shapes=[
            pltpu.VMEM((8, coefs, width), jnp.float32),
            pltpu.VMEM((deep, width), jnp.float32),
            pltpu.VMEM((parts, 8, 128), jnp.float32),
            pltpu.VMEM((coefs, width), jnp.float32),
            pltpu.VMEM((coefs, width), jnp.float32),
            pltpu.SemaphoreType.DMA((7,)),
        ]
        + move,
        input_output_aliases={6: 1, 7: 2, 8: 3, 9: 4},
        compiler_params=pltpu.CompilerParams(vmem_limit_bytes=52 << 20),
        name="face",
    )(slot_of, stage_of, pair_row[0], late, pair_weight[0], early, chain, packed, top, bottom)
    (updated,) = section(chain, *halos(packed, top, bottom), False)
    return face.reshape(coefs, 8, width), updated.reshape(stator_field.shape)


def solution(mesh):
    placed = (
        P("span", "rows", None, None),
        P("span", "rows", None),
        P("span", "rows"),
        P("span", "rows"),
        P("span", "rows", None, None),
        P(None, None, "span", "rows"),
        P("span", "rows"),
    )

    return jax.shard_map(
        per_device,
        mesh=mesh,
        in_specs=placed,
        out_specs=(P(None, "span", "rows"), P(None, None, "span", "rows")),
        check_vma=False,
    )
```
